768 devices in a mesh: sensor: 48 (over y_lo, z), param: 16 (over y_hi, x, core).
Axes of the slice: x: 4, y: 8 (y_hi: 2, y_lo: 4; y = y_hi * 4 + y_lo), z: 12, core: 2. Of those that a mesh axis runs over, the one named last changes fastest.
Arguments:
- parameter_field: float32 [8, 768, 420], P(None, ('param', 'sensor')), may hold values from -6 to 6
- operator_blocks: float32 [2, 421, 48, 16, 384], P(None, None, 'sensor', 'param'), may hold values from -0.5 to 0.5
- noise_weights: float32 [384, 420], P('sensor'), may hold values from 0.25 to 4
Outputs:
- hessian_action: float32 [8, 768, 420], P(None, ('param', 'sensor'))
The draws below stay inside these ranges and needn't reach their ends.
All inputs are finite; a program needn't handle non-finite values.
Results may differ from the reference program's by a relative error of at most 0.000071.
Values sent between devices are 32-bit elements; how exact they have to be, the bound alone decides.
No kernel may reach another device: no remote copies, remote signals or barrier semaphores. Data moves between devices by JAX's collectives and lax.ppermute only.
A program may use at most 64 MiB of HBM per device.

```python
import math
import jax
import jax.numpy as jnp
from jax import lax

NT = 420
NF = 421
SENS_DEV = 8
PAR_DEV = 48
NVEC = 8
SENSORS = 384
PARAMS = 768
N_SENSOR = 48
N_PARAM = 16


def with_spikes(values, own_key, source, target, parts, factor):
    def block_of(position):
        return (jnp.arange(values.shape[position]) // (values.shape[position] // parts)).reshape((-1,) + (1,) * (values.ndim - 1 - position))

    first = jax.random.permutation(own_key, parts)[block_of(target)]
    second = (block_of(target) + parts // 2) % parts
    return jnp.where((block_of(source) == first) | (block_of(source) == second), factor * values, values)


def levels(key, shape, shards, least, high):
    def one(position, parts):
        steps = jax.random.uniform(jax.random.fold_in(jax.random.fold_in(key, 6), position), (parts,), jnp.float32, least / len(shards), high / len(shards))
        return jnp.repeat(jnp.exp(steps), shape[position] // parts).reshape((-1,) + (1,) * (len(shape) - position - 1))

    factor_of = one(*shards[0])
    for cut in shards[1:]:
        factor_of = factor_of * one(*cut)
    return factor_of


def gaussian(own_key, shape, deviation, most, cuts=(), held_as=jnp.bfloat16):
    level = levels(own_key, shape, cuts, -0.22, 0.18) if cuts else 1.0
    entries = jax.random.normal(own_key, shape, jnp.float32) * deviation * level
    return jnp.minimum(jnp.maximum(entries, -most), most).astype(held_as)


def heavy_noise(rng, dims, deviation, reach, pieces, heavy, kind=jnp.bfloat16):
    drawn = deviation * jax.random.normal(rng, dims, jnp.float32)
    if pieces:
        drawn = drawn * levels(rng, dims, pieces, -0.22, 0.18)
    return jnp.clip(with_spikes(drawn, jax.random.fold_in(rng, 3), *heavy), -reach, reach).astype(kind)


def setup_inputs(seed: int = 0) -> dict:
    arg_keys = jax.random.split(jax.random.key(seed), 4)
    parameter_field = gaussian(arg_keys[0], (NVEC, PARAMS, NT), 1.0, 6.0, ((1, 768),), jnp.float32)
    operator_blocks = heavy_noise(arg_keys[1], (2, NF, N_SENSOR, N_PARAM, PAR_DEV * SENS_DEV), PARAMS ** -0.5, 0.5, ((2, 48), (3, 16)), (2, 4, 48, 3.25), jnp.float32)
    noise_weights = jnp.clip(jnp.exp(math.log(4.0) - 2.7725887 * jax.random.uniform(arg_keys[2], (SENSORS, NT), jnp.float32) ** levels(arg_keys[2], (SENSORS, NT), ((0, 48),), -0.2, 0.2)), 0.25, 4.0)
    return {"parameter_field": parameter_field, "operator_blocks": operator_blocks, "noise_weights": noise_weights}


highest = lax.Precision.HIGHEST


def product(form, left, right):
    return jnp.einsum(form, left, right, precision=highest)


def reference(parameter_field, operator_blocks, noise_weights):
    length = 2 * NT
    tiled = operator_blocks.reshape(2, NF, N_SENSOR, N_PARAM, PAR_DEV, SENS_DEV)
    whole_blocks = jnp.transpose(tiled, (0, 1, 2, 5, 3, 4)).reshape(2, NF, SENSORS, PARAMS)
    real_blocks = whole_blocks[0]
    imag_blocks = whole_blocks[1]
    spectrum = jnp.fft.rfft(parameter_field, n=length, axis=-1)
    field_real = jnp.transpose(jnp.real(spectrum), (2, 0, 1))
    field_imag = jnp.transpose(jnp.imag(spectrum), (2, 0, 1))
    pred_real = product("ksp,kvp->kvs", real_blocks, field_real) - product("ksp,kvp->kvs", imag_blocks, field_imag)
    pred_imag = product("ksp,kvp->kvs", real_blocks, field_imag) + product("ksp,kvp->kvs", imag_blocks, field_real)
    predicted = lax.complex(jnp.transpose(pred_real, (1, 2, 0)), jnp.transpose(pred_imag, (1, 2, 0)))
    data = jnp.fft.irfft(predicted, n=length, axis=-1)[..., :NT]
    weighted = data * noise_weights[None, :, :]
    weighted_spectrum = jnp.fft.rfft(weighted, n=length, axis=-1)
    data_real = jnp.transpose(jnp.real(weighted_spectrum), (2, 0, 1))
    data_imag = jnp.transpose(jnp.imag(weighted_spectrum), (2, 0, 1))
    adj_real = product("ksp,kvs->kvp", real_blocks, data_real) + product("ksp,kvs->kvp", imag_blocks, data_imag)
    adj_imag = product("ksp,kvs->kvp", real_blocks, data_imag) - product("ksp,kvs->kvp", imag_blocks, data_real)
    adjoint_spectrum = lax.complex(jnp.transpose(adj_real, (1, 2, 0)), jnp.transpose(adj_imag, (1, 2, 0)))
    return jnp.fft.irfft(adjoint_spectrum, n=length, axis=-1)[..., :NT]
```

```python
import functools
import math

import jax
import jax.numpy as jnp
import numpy as np
from jax import lax
from jax.experimental import pallas as pl
from jax.experimental.pallas import tpu as pltpu
from jax.sharding import Mesh
from jax.sharding import PartitionSpec as P

LANES = 128
VMEM_BYTES = 16 << 20
NATURAL = ("y_lo", "z", "y_hi", "x", "core")


def tables(time_steps, width):
    length = 2 * time_steps
    index = np.arange(time_steps + 1)
    angles = (index[:, None] * index[None, :] % length) * (2.0 * math.pi / length)
    out = []
    for values in (np.cos(angles), -np.sin(angles)):
        full = np.zeros((width, width), np.float64)
        full[: time_steps + 1, : time_steps + 1] = values
        high = full.astype(jnp.bfloat16)
        low = (full - high.astype(np.float64)).astype(jnp.bfloat16)
        out += [high, low]
    factor = np.zeros((1, width), np.float32)
    factor[0, : time_steps + 1] = 2.0 / length
    factor[0, 0] = factor[0, time_steps] = 1.0 / length
    return out, factor


def dot3(left, high, low):
    left_high = left.astype(jnp.bfloat16)
    left_low = (left - left_high.astype(jnp.float32)).astype(jnp.bfloat16)
    dot = functools.partial(jnp.dot, preferred_element_type=jnp.float32)
    return dot(left_high, high) + (dot(left_high, low) + dot(left_low, high))


def flip_kernel(freq_count, f_ref, out_ref, tail_ref):
    groups = f_ref.shape[0] // (2 * freq_count)
    whole = freq_count // LANES
    left = freq_count - whole * LANES
    tail_ref[left:, :] = jnp.zeros_like(tail_ref[left:, :])
    for c in range(2):
        for j in range(groups):
            rows = slice(j * LANES, (j + 1) * LANES)
            for i in range(whole + 1):
                count = LANES if i < whole else left
                first = (c * freq_count + i * LANES) * groups + j
                block = f_ref[pl.ds(first, count, stride=groups), :]
                if i == whole:
                    tail_ref[:left, :] = block
                    block = tail_ref[...]
                out_ref[c, rows, i * LANES : (i + 1) * LANES] = block.T


def forward_kernel(
    n_y, x0, x1, x2, x3, f_ref, ch, cl, sh, sl, factor, keep_ref, send_ref, xf_ref, p_ref
):
    y = lax.axis_index("y_lo")
    core = lax.axis_index("core")
    block_rows, width = x0.shape
    sens = p_ref.shape[1] // 8
    for k, x_ref in enumerate((x0, x1, x2, x3)[:n_y]):
        x = x_ref[...]
        rows = slice(k * block_rows, (k + 1) * block_rows)
        xf_ref[0, rows, :] = dot3(x, ch[...], cl[...])
        xf_ref[1, rows, :] = dot3(x, sh[...], sl[...])
    for lane in range(0, width, LANES):
        lanes = slice(lane, lane + LANES)
        acc = tuple(jnp.zeros((8, LANES), jnp.float32) for _ in range(2 * sens))
        for k in range(n_y):
            base = lax.rem(y + n_y - k, n_y) * block_rows

            def body(q, acc, k=k, base=base):
                row = pl.multiple_of(k * block_rows + q * 8, 8)
                xr = xf_ref[0, pl.ds(row, 8), lanes]
                xi = xf_ref[1, pl.ds(row, 8), lanes]
                start = pl.multiple_of(base + q * 8, 8)
                fr_tile = f_ref[0, pl.ds(start, 8), lanes]
                fi_tile = f_ref[1, pl.ds(start, 8), lanes]
                out = []
                for r in range(sens):
                    fr = jnp.broadcast_to(fr_tile[r : r + 1, :], (8, LANES))
                    fi = jnp.broadcast_to(fi_tile[r : r + 1, :], (8, LANES))
                    out.append(acc[2 * r] + (fr * xr - fi * xi))
                    out.append(acc[2 * r + 1] + (fr * xi + fi * xr))
                return tuple(out)

            acc = lax.fori_loop(0, block_rows // 8, body, acc, unroll=2)
        scale = factor[:, lanes]
        for r in range(sens):
            p_ref[0, r * 8 : r * 8 + 8, lanes] = acc[2 * r] * scale
            p_ref[1, r * 8 : r * 8 + 8, lanes] = acc[2 * r + 1] * scale
    xf_ref[0, : sens * 8, :] = dot3(p_ref[0], ch[...], cl[...]) + dot3(p_ref[1], sh[...], sl[...])
    half = sens * 4
    keep_ref[...] = xf_ref[0, pl.ds(pl.multiple_of(core * half, 8), half), :]
    send_ref[...] = xf_ref[0, pl.ds(pl.multiple_of((1 - core) * half, 8), half), :]


def adjoint_kernel(
    n_y, mine_ref, other_ref, noise_ref, f_ref, ch, cl, sh, sl, factor, o0, o1, o2, o3, d_ref, w_ref, g_ref
):
    y = lax.axis_index("y_lo")
    core = lax.axis_index("core")
    half, width = mine_ref.shape
    sens = half // 4
    block_rows = o0.shape[0]
    d_ref[pl.ds(pl.multiple_of(core * half, 8), half), :] = mine_ref[...]
    d_ref[pl.ds(pl.multiple_of((1 - core) * half, 8), half), :] = other_ref[...]
    for r in range(sens):
        rows = slice(r * 8, r * 8 + 8)
        d_ref[rows, :] = d_ref[rows, :] * noise_ref[r : r + 1, :]
    weighted = d_ref[...]
    w_ref[0] = dot3(weighted, ch[...], cl[...]) * factor[...]
    w_ref[1] = dot3(weighted, sh[...], sl[...]) * factor[...]
    for lane in range(0, width, LANES):
        lanes = slice(lane, lane + LANES)
        wr = [w_ref[0, r * 8 : r * 8 + 8, lanes] for r in range(sens)]
        wi = [w_ref[1, r * 8 : r * 8 + 8, lanes] for r in range(sens)]
        for k in range(n_y):
            base = lax.rem(y + k, n_y) * block_rows

            def body(q, carry, k=k, base=base):
                start = pl.multiple_of(base + q * 8, 8)
                fr_tile = f_ref[0, pl.ds(start, 8), lanes]
                fi_tile = f_ref[1, pl.ds(start, 8), lanes]
                gr = jnp.zeros((8, LANES), jnp.float32)
                gi = jnp.zeros((8, LANES), jnp.float32)
                for r in range(sens):
                    fr = jnp.broadcast_to(fr_tile[r : r + 1, :], (8, LANES))
                    fi = jnp.broadcast_to(fi_tile[r : r + 1, :], (8, LANES))
                    gr = gr + (fr * wr[r] + fi * wi[r])
                    gi = gi + (fr * wi[r] - fi * wr[r])
                row = pl.multiple_of(k * block_rows + q * 8, 8)
                g_ref[0, pl.ds(row, 8), lanes] = gr
                g_ref[1, pl.ds(row, 8), lanes] = gi
                return carry

            lax.fori_loop(0, block_rows // 8, body, 0, unroll=2)
    for k, o_ref in enumerate((o0, o1, o2, o3)[:n_y]):
        rows = slice(k * block_rows, (k + 1) * block_rows)
        o_ref[...] = dot3(g_ref[0, rows, :], ch[...], cl[...]) + dot3(
            g_ref[1, rows, :], sh[...], sl[...]
        )


def shift(n, k):
    return [(i, (i + k) % n) for i in range(n)]


def shards(sizes, parameter_field, operator_blocks, noise_weights):
    n_y, n_z, n_yh, n_x, n_core = sizes
    vectors, _, time_steps = parameter_field.shape
    sens = noise_weights.shape[0]
    freq_count = time_steps + 1
    width = -(-freq_count // LANES) * LANES
    pairs = operator_blocks.shape[4]
    block_rows = n_z * vectors
    (ch, cl, sh, sl), factor = tables(time_steps, width)
    consts = (jnp.asarray(ch), jnp.asarray(cl), jnp.asarray(sh), jnp.asarray(sl), jnp.asarray(factor))
    f32 = jnp.float32
    params = pltpu.CompilerParams(vmem_limit_bytes=VMEM_BYTES)
    pad = width - time_steps

    own = jnp.pad(parameter_field.reshape(vectors, time_steps), ((0, 0), (0, pad)))
    noise = jnp.pad(noise_weights, ((0, 0), (0, pad)))
    spread = jnp.broadcast_to(own[None], (n_z, vectors, width))
    column = lax.all_to_all(spread, "z", 0, 0, tiled=True).reshape(block_rows, width)
    blocks = [column] + [lax.ppermute(column, "y_lo", shift(n_y, k)) for k in range(1, n_y)]

    flipped = pl.pallas_call(
        functools.partial(flip_kernel, freq_count),
        out_shape=jax.ShapeDtypeStruct((2, pairs, width), f32),
        scratch_shapes=[pltpu.VMEM((LANES, LANES), f32)],
        compiler_params=params,
        name="flip",
    )(operator_blocks.reshape(2 * freq_count * pairs // LANES, LANES))

    half = jax.ShapeDtypeStruct((sens * vectors // 2, width), f32)
    keep, send = pl.pallas_call(
        functools.partial(forward_kernel, n_y),
        out_shape=(half, half),
        scratch_shapes=[
            pltpu.VMEM((2, n_y * block_rows, width), f32),
            pltpu.VMEM((2, sens * vectors, width), f32),
        ],
        compiler_params=params,
        name="forward",
    )(*blocks, flipped, *consts)

    total = keep + lax.ppermute(send, "core", shift(n_core, 1))
    received = [lax.ppermute(total, "x", shift(n_x, k)) for k in range(1, n_x)]
    total = sum(received, total)
    total = total + lax.ppermute(total, "y_hi", shift(n_yh, 1))
    other = lax.ppermute(total, "core", shift(n_core, 1))

    block = jax.ShapeDtypeStruct((block_rows, width), f32)
    parts = pl.pallas_call(
        functools.partial(adjoint_kernel, n_y),
        out_shape=(block,) * n_y,
        scratch_shapes=[
            pltpu.VMEM((sens * vectors, width), f32),
            pltpu.VMEM((2, sens * vectors, width), f32),
            pltpu.VMEM((2, n_y * block_rows, width), f32),
        ],
        compiler_params=params,
        name="adjoint",
    )(total, other, noise, flipped, *consts)

    moved = [lax.ppermute(parts[k], "y_lo", shift(n_y, k)) for k in range(1, n_y)]
    summed = sum(moved, parts[0]).reshape(n_z, vectors, width)
    mine = lax.all_to_all(summed, "z", 0, 0, tiled=True)
    return jnp.sum(mine, axis=0)[:, :time_steps].reshape(vectors, 1, time_steps)


def build(mesh, sizes):
    natural = Mesh(mesh.devices.reshape(sizes), NATURAL)
    sensor, param = NATURAL[:2], NATURAL[2:]
    in_specs = (
        P(None, param + sensor, None),
        P(None, None, sensor, param, None),
        P(sensor, None),
    )
    out_specs = P(None, param + sensor, None)
    return jax.shard_map(
        functools.partial(shards, sizes),
        mesh=natural,
        in_specs=in_specs,
        out_specs=out_specs,
        check_vma=False,
    )


def solution(mesh):
    return build(mesh, (4, 12, 2, 4, 2))
```

```python
import functools
import math

import jax
import jax.numpy as jnp
import numpy as np
from jax import lax
from jax.experimental import pallas as pl
from jax.experimental.pallas import tpu as pltpu
from jax.sharding import Mesh
from jax.sharding import PartitionSpec as P

LANES = 128
VMEM_BYTES = 16 << 20
NATURAL = ("y_lo", "z", "y_hi", "x", "core")


def tables(time_steps, width):
    length = 2 * time_steps
    index = np.arange(time_steps + 1)
    angles = (index[:, None] * index[None, :] % length) * (2.0 * math.pi / length)
    out = []
    for values in (np.cos(angles), -np.sin(angles)):
        full = np.zeros((width, width), np.float64)
        full[: time_steps + 1, : time_steps + 1] = values
        high = full.astype(jnp.bfloat16)
        low = (full - high.astype(np.float64)).astype(jnp.bfloat16)
        out += [high, low]
    factor = np.zeros((1, width), np.float32)
    factor[0, : time_steps + 1] = 2.0 / length
    factor[0, 0] = factor[0, time_steps] = 1.0 / length
    return out, factor


def dot3(left, high, low):
    left_high = left.astype(jnp.bfloat16)
    left_low = (left - left_high.astype(jnp.float32)).astype(jnp.bfloat16)
    dot = functools.partial(jnp.dot, preferred_element_type=jnp.float32)
    return dot(left_high, high) + (dot(left_high, low) + dot(left_low, high))


def tail_plan(rows, time_steps):
    left = time_steps % LANES
    groups = max(g for g in range(1, LANES // left + 1) if rows % (8 * g) == 0)
    return left, groups, rows // groups


def packed_rows(rows, time_steps):
    return rows * (time_steps // LANES) + tail_plan(rows, time_steps)[2]


def pack(value, out_ref, time_steps):
    rows = value.shape[0]
    whole = time_steps // LANES
    left, groups, height = tail_plan(rows, time_steps)
    for j in range(whole):
        out_ref[j * rows : (j + 1) * rows, :] = value[:, j * LANES : (j + 1) * LANES]
    lane = lax.broadcasted_iota(jnp.int32, (height, LANES), 1)
    tail = jnp.zeros((height, LANES), jnp.float32)
    for g in range(groups):
        piece = value[g * height : (g + 1) * height, whole * LANES :]
        if g:
            piece = pltpu.roll(piece, g * left, 1)
        tail = jnp.where((lane >= g * left) & (lane < (g + 1) * left), piece, tail)
    out_ref[whole * rows :, :] = tail


def unpack(packed, rows, time_steps):
    whole = time_steps // LANES
    left, groups, height = tail_plan(rows, time_steps)
    lane = lax.broadcasted_iota(jnp.int32, (height, LANES), 1)
    tail = packed[whole * rows :, :]
    pieces = []
    for g in range(groups):
        piece = pltpu.roll(tail, LANES - g * left, 1) if g else tail
        pieces.append(jnp.where(lane < left, piece, 0.0))
    tiles = [packed[j * rows : (j + 1) * rows, :] for j in range(whole)]
    return jnp.concatenate(tiles + [jnp.concatenate(pieces, axis=0)], axis=1)


def pack_kernel(time_steps, x_ref, out_ref):
    pack(x_ref[...], out_ref, time_steps)


def unpack_sum_kernel(time_steps, *refs):
    out_ref = refs[-1]
    total = refs[0][...]
    for ref in refs[1:-1]:
        total = total + ref[...]
    out_ref[...] = unpack(total, out_ref.shape[0], time_steps)


def flip_kernel(freq_count, f_hbm, out_ref, f_ref, tail_ref, sem):
    copy = pltpu.make_async_copy(f_hbm.at[:, 0, :], f_ref, sem)
    copy.start()
    groups = f_ref.shape[0] // (2 * freq_count)
    whole = freq_count // LANES
    left = freq_count - whole * LANES
    tail_ref[left:, :] = jnp.zeros_like(tail_ref[left:, :])
    copy.wait()
    for c in range(2):
        for j in range(groups):
            rows = slice(j * LANES, (j + 1) * LANES)
            for i in range(whole + 1):
                count = LANES if i < whole else left
                first = (c * freq_count + i * LANES) * groups + j
                block = f_ref[pl.ds(first, count, stride=groups), :]
                if i == whole:
                    tail_ref[:left, :] = block
                    block = tail_ref[...]
                out_ref[c, rows, i * LANES : (i + 1) * LANES] = block.T


def transform(x, rows, xf_ref, tabs):
    ch, cl, sh, sl = tabs
    xf_ref[0, rows, :] = dot3(x, ch[...], cl[...])
    xf_ref[1, rows, :] = dot3(x, sh[...], sl[...])


def inverse(re, im, tabs):
    ch, cl, sh, sl = tabs
    return dot3(re, ch[...], cl[...]) + dot3(im, sh[...], sl[...])


def sums(xf_ref, f_ref, blocks, block_rows, sensors, acc, lanes):
    for first, base in blocks:

        def body(q, acc, first=first, base=base):
            row = pl.multiple_of(first + q * 8, 8)
            xr = xf_ref[0, pl.ds(row, 8), lanes]
            xi = xf_ref[1, pl.ds(row, 8), lanes]
            start = pl.multiple_of(base + q * 8, 8)
            fr_tile = f_ref[0, pl.ds(start, 8), lanes]
            fi_tile = f_ref[1, pl.ds(start, 8), lanes]
            out = []
            for i, r in enumerate(sensors):
                fr = jnp.broadcast_to(fr_tile[r : r + 1, :], (8, LANES))
                fi = jnp.broadcast_to(fi_tile[r : r + 1, :], (8, LANES))
                out.append(acc[2 * i] + (fr * xr - fi * xi))
                out.append(acc[2 * i + 1] + (fr * xi + fi * xr))
            return tuple(out)

        acc = lax.fori_loop(0, block_rows // 8, body, acc, unroll=2)
    return acc


def lane_tiles(width):
    return [slice(lane, lane + LANES) for lane in range(0, width, LANES)]


def first_kernel(n_y, x_ref, f_ref, ch, cl, sh, sl, acc_ref, xf_ref):
    block_rows, width = x_ref.shape
    sens = acc_ref.shape[1] // 8
    transform(x_ref[...], slice(0, block_rows), xf_ref, (ch, cl, sh, sl))
    base = lax.axis_index("y_lo") * block_rows
    for lanes in lane_tiles(width):
        acc = tuple(jnp.zeros((8, LANES), jnp.float32) for _ in range(2 * sens))
        acc = sums(xf_ref, f_ref, [(0, base)], block_rows, range(sens), acc, lanes)
        for r in range(sens):
            acc_ref[0, r * 8 : r * 8 + 8, lanes] = acc[2 * r]
            acc_ref[1, r * 8 : r * 8 + 8, lanes] = acc[2 * r + 1]


def half_series(n_y, block_rows, time_steps, sensors, acc_ref, xf_ref, f_ref, tabs, factor, out_ref, p_ref):
    y = lax.axis_index("y_lo")
    blocks = [
        ((k - 1) * block_rows, lax.rem(y + n_y - k, n_y) * block_rows) for k in range(1, n_y)
    ]
    for lanes in lane_tiles(p_ref.shape[2]):
        acc = []
        for r in sensors:
            acc += [acc_ref[0, r * 8 : r * 8 + 8, lanes], acc_ref[1, r * 8 : r * 8 + 8, lanes]]
        acc = sums(xf_ref, f_ref, blocks, block_rows, sensors, tuple(acc), lanes)
        scale = factor[:, lanes]
        for i in range(len(sensors)):
            p_ref[0, i * 8 : i * 8 + 8, lanes] = acc[2 * i] * scale
            p_ref[1, i * 8 : i * 8 + 8, lanes] = acc[2 * i + 1] * scale
    pack(inverse(p_ref[0], p_ref[1], tabs), out_ref, time_steps)


def halves(sens, core, do):
    half = sens // 2
    for c in range(2):
        pl.when(core == c)(lambda c=c: do(range(c * half, (c + 1) * half)))


def send_kernel(n_y, block_rows, time_steps, *refs):
    xs = refs[: n_y - 1]
    acc_ref, f_ref, ch, cl, sh, sl, factor, out_ref, xf_ref, p_ref = refs[n_y - 1 :]
    tabs = (ch, cl, sh, sl)
    for k, x_ref in enumerate(xs):
        x = unpack(x_ref[...], block_rows, time_steps)
        transform(x, slice(k * block_rows, (k + 1) * block_rows), xf_ref, tabs)
    sens = acc_ref.shape[1] // 8
    halves(
        sens,
        1 - lax.axis_index("core"),
        lambda sensors: half_series(
            n_y, block_rows, time_steps, sensors, acc_ref, xf_ref, f_ref, tabs, factor, out_ref, p_ref
        ),
    )


def keep_kernel(n_y, block_rows, time_steps, xf_ref, acc_ref, f_ref, ch, cl, sh, sl, factor, out_ref, p_ref):
    sens = acc_ref.shape[1] // 8
    halves(
        sens,
        lax.axis_index("core"),
        lambda sensors: half_series(
            n_y, block_rows, time_steps, sensors, acc_ref, xf_ref, f_ref, (ch, cl, sh, sl), factor, out_ref, p_ref
        ),
    )


def weigh(sensors, d_ref, noise_ref, tabs, factor, w_ref, scratch, time_steps):
    data = unpack(d_ref[...], len(sensors) * 8, time_steps)
    for i, r in enumerate(sensors):
        rows = slice(i * 8, i * 8 + 8)
        scratch[rows, :] = data[rows, :] * noise_ref[r : r + 1, :]
    ch, cl, sh, sl = tabs
    w_ref[0] = dot3(scratch[...], ch[...], cl[...]) * factor[...]
    w_ref[1] = dot3(scratch[...], sh[...], sl[...]) * factor[...]


def products(sensors, w_ref, f_ref, base, count, lanes, start_of, out):
    wr = [w_ref[0, i * 8 : i * 8 + 8, lanes] for i in range(len(sensors))]
    wi = [w_ref[1, i * 8 : i * 8 + 8, lanes] for i in range(len(sensors))]

    def body(q, carry):
        start = pl.multiple_of(base + q * 8, 8)
        fr_tile = f_ref[0, pl.ds(start, 8), lanes]
        fi_tile = f_ref[1, pl.ds(start, 8), lanes]
        gr, gi = start_of(start)
        for i, r in enumerate(sensors):
            fr = jnp.broadcast_to(fr_tile[r : r + 1, :], (8, LANES))
            fi = jnp.broadcast_to(fi_tile[r : r + 1, :], (8, LANES))
            gr = gr + (fr * wr[i] + fi * wi[i])
            gi = gi + (fr * wi[i] - fi * wr[i])
        out(q, gr, gi)
        return carry

    lax.fori_loop(0, count, body, 0, unroll=2)


def mine_kernel(time_steps, d_ref, noise_ref, f_ref, ch, cl, sh, sl, factor, g_ref, w_ref, scratch):
    sens = noise_ref.shape[0]

    def do(sensors):
        weigh(sensors, d_ref, noise_ref, (ch, cl, sh, sl), factor, w_ref, scratch, time_steps)
        for lanes in lane_tiles(g_ref.shape[2]):

            def out(q, gr, gi, lanes=lanes):
                row = pl.multiple_of(q * 8, 8)
                g_ref[0, pl.ds(row, 8), lanes] = gr
                g_ref[1, pl.ds(row, 8), lanes] = gi

            zero = jnp.zeros((8, LANES), jnp.float32)
            products(sensors, w_ref, f_ref, 0, g_ref.shape[1] // 8, lanes, lambda s: (zero, zero), out)

    halves(sens, lax.axis_index("core"), do)


def weigh_kernel(time_steps, d_ref, noise_ref, ch, cl, sh, sl, factor, w_ref, scratch):
    halves(
        noise_ref.shape[0],
        1 - lax.axis_index("core"),
        lambda sensors: weigh(sensors, d_ref, noise_ref, (ch, cl, sh, sl), factor, w_ref, scratch, time_steps),
    )


def part_kernel(n_y, k, time_steps, w_ref, g_ref, f_ref, ch, cl, sh, sl, out_ref, h_ref):
    block_rows = h_ref.shape[1]
    base = lax.rem(lax.axis_index("y_lo") + k, n_y) * block_rows

    def do(sensors):
        for lanes in lane_tiles(h_ref.shape[2]):

            def out(q, gr, gi, lanes=lanes):
                row = pl.multiple_of(q * 8, 8)
                h_ref[0, pl.ds(row, 8), lanes] = gr
                h_ref[1, pl.ds(row, 8), lanes] = gi

            def start_of(start, lanes=lanes):
                return g_ref[0, pl.ds(start, 8), lanes], g_ref[1, pl.ds(start, 8), lanes]

            products(sensors, w_ref, f_ref, base, block_rows // 8, lanes, start_of, out)

    halves(w_ref.shape[1] // 4, 1 - lax.axis_index("core"), do)
    pack(inverse(h_ref[0], h_ref[1], (ch, cl, sh, sl)), out_ref, time_steps)


def shift(n, k):
    return [(i, (i + k) % n) for i in range(n)]


def shards(sizes, parameter_field, operator_blocks, noise_weights):
    n_y, n_z, n_yh, n_x, n_core = sizes
    vectors, _, time_steps = parameter_field.shape
    sens = noise_weights.shape[0]
    freq_count = time_steps + 1
    width = -(-freq_count // LANES) * LANES
    pairs = operator_blocks.shape[4]
    block_rows = n_z * vectors
    (ch, cl, sh, sl), factor = tables(time_steps, width)
    consts = (jnp.asarray(ch), jnp.asarray(cl), jnp.asarray(sh), jnp.asarray(sl), jnp.asarray(factor))
    f32 = jnp.float32
    params = pltpu.CompilerParams(vmem_limit_bytes=VMEM_BYTES)
    pad = width - time_steps

    own = jnp.pad(parameter_field.reshape(vectors, time_steps), ((0, 0), (0, pad)))
    noise = jnp.pad(noise_weights, ((0, 0), (0, pad)))
    spread = jnp.broadcast_to(own[None], (n_z, vectors, width))
    column = lax.all_to_all(spread, "z", 0, 0, tiled=True).reshape(block_rows, width)

    def call(kernel, name, out, *operands, scratch=(), **options):
        return pl.pallas_call(
            kernel,
            out_shape=out,
            scratch_shapes=[pltpu.VMEM(shape, f32) for shape in scratch],
            compiler_params=params,
            name=name,
        )(*operands)

    def of(*shape):
        return jax.ShapeDtypeStruct(shape, f32)

    tabs, factor = consts[:4], consts[4]
    half_rows = sens * vectors // 2
    packed_block = of(packed_rows(block_rows, time_steps), LANES)
    packed_half = of(packed_rows(half_rows, time_steps), LANES)

    flat_rows = 2 * freq_count * pairs // LANES
    flipped = pl.pallas_call(
        functools.partial(flip_kernel, freq_count),
        out_shape=of(2, pairs, width),
        in_specs=[pl.BlockSpec(memory_space=pl.ANY)],
        scratch_shapes=[
            pltpu.VMEM((flat_rows, LANES), f32),
            pltpu.VMEM((LANES, LANES), f32),
            pltpu.SemaphoreType.DMA,
        ],
        compiler_params=params,
        name="flip",
    )(operator_blocks.reshape(flat_rows, 1, LANES))

    packed = call(functools.partial(pack_kernel, time_steps), "pack", packed_block, column)
    blocks = [lax.ppermute(packed, "y_lo", shift(n_y, k)) for k in range(1, n_y)]
    acc = call(
        functools.partial(first_kernel, n_y),
        "first",
        of(2, sens * vectors, width),
        column,
        flipped,
        *tabs,
        scratch=[(2, block_rows, width)],
    )
    send, spectrum = call(
        functools.partial(send_kernel, n_y, block_rows, time_steps),
        "send",
        (packed_half, of(2, (n_y - 1) * block_rows, width)),
        *blocks,
        acc,
        flipped,
        *consts,
        scratch=[(2, half_rows, width)],
    )
    sent = lax.ppermute(send, "core", shift(n_core, 1))
    keep = call(
        functools.partial(keep_kernel, n_y, block_rows, time_steps),
        "keep",
        packed_half,
        spectrum,
        acc,
        flipped,
        *consts,
        scratch=[(2, half_rows, width)],
    )

    total = keep + sent
    received = [lax.ppermute(total, "x", shift(n_x, k)) for k in range(1, n_x)]
    total = sum(received, total)
    total = total + lax.ppermute(total, "y_hi", shift(n_yh, 1))
    other = lax.ppermute(total, "core", shift(n_core, 1))

    partial_spectrum = call(
        functools.partial(mine_kernel, time_steps),
        "mine",
        of(2, pairs, width),
        total,
        noise,
        flipped,
        *consts,
        scratch=[(2, half_rows, width), (half_rows, width)],
    )
    weighted = call(
        functools.partial(weigh_kernel, time_steps),
        "weigh",
        of(2, half_rows, width),
        other,
        noise,
        *consts,
        scratch=[(half_rows, width)],
    )
    moved = []
    for k in [*range(n_y - 1, 0, -1), 0]:
        part = call(
            functools.partial(part_kernel, n_y, k, time_steps),
            f"part{k}",
            packed_block,
            weighted,
            partial_spectrum,
            flipped,
            *tabs,
            scratch=[(2, block_rows, width)],
        )
        moved.append(lax.ppermute(part, "y_lo", shift(n_y, k)) if k else part)
    summed = call(
        functools.partial(unpack_sum_kernel, time_steps), "gathered", of(block_rows, width), *moved
    ).reshape(n_z, vectors, width)
    mine = lax.all_to_all(summed, "z", 0, 0, tiled=True)
    return jnp.sum(mine, axis=0)[:, :time_steps].reshape(vectors, 1, time_steps)


def build(mesh, sizes):
    natural = Mesh(mesh.devices.reshape(sizes), NATURAL)
    sensor, param = NATURAL[:2], NATURAL[2:]
    in_specs = (
        P(None, param + sensor, None),
        P(None, None, sensor, param, None),
        P(sensor, None),
    )
    out_specs = P(None, param + sensor, None)
    return jax.shard_map(
        functools.partial(shards, sizes),
        mesh=natural,
        in_specs=in_specs,
        out_specs=out_specs,
        check_vma=False,
    )


def solution(mesh):
    return build(mesh, (4, 12, 2, 4, 2))
```
